32 devices in a mesh: seq: 4 (over y, core), fsdp: 8 (over z, x).
Axes of the slice: x: 2, y: 2, z: 4, core: 2. Of those that a mesh axis runs over, the one named last changes fastest.
Arguments:
- latents: bfloat16 [8, 512, 1152], P('fsdp', 'seq'), may hold values from -6 to 6
- conditioning: float32 [8, 1152], P('fsdp'), may hold values from -6 to 6
- modulation_weight: bfloat16 [1, 1152, 6912], P(None, 'fsdp'), may hold values from -0.1875 to 0.1875
- modulation_bias: bfloat16 [1, 6912], P(None, 'fsdp'), may hold values from -3 to 3
- qkv_weight: bfloat16 [1, 1152, 3456], P(None, 'fsdp'), may hold values from -1 to 1
- qkv_bias: bfloat16 [1, 2304], P(None, 'fsdp'), may hold values from -3 to 3
- proj_weight: bfloat16 [1, 1152, 1152], P(None, 'fsdp'), may hold values from -4 to 4
- proj_bias: bfloat16 [1, 1152], P(None, 'fsdp'), may hold values from -3 to 3
- fc1_weight: bfloat16 [1, 1152, 4608], P(None, 'fsdp'), may hold values from -0.1875 to 0.1875
- fc1_bias: bfloat16 [1, 4608], P(None, 'fsdp'), may hold values from -3 to 3
- fc2_weight: bfloat16 [1, 4608, 1152], P(None, 'fsdp'), may hold values from -0.09375 to 0.09375
- fc2_bias: bfloat16 [1, 1152], P(None, 'fsdp'), may hold values from -3 to 3
- cotangent: float32 [8, 512, 1152], P('fsdp', 'seq'), may hold values from -6 to 6
Outputs:
- block_output: float32 [8, 512, 1152], P('fsdp', 'seq')
- latents_grad: float32 [8, 512, 1152], P('fsdp', 'seq')
- conditioning_grad: float32 [8, 1152], P('fsdp')
- modulation_weight_grad: float32 [1, 1152, 6912], P(None, 'fsdp')
- modulation_bias_grad: float32 [1, 6912], P(None, 'fsdp')
- qkv_weight_grad: float32 [1, 1152, 3456], P(None, 'fsdp')
- qkv_bias_grad: float32 [1, 2304], P(None, 'fsdp')
- proj_weight_grad: float32 [1, 1152, 1152], P(None, 'fsdp')
- proj_bias_grad: float32 [1, 1152], P(None, 'fsdp')
- fc1_weight_grad: float32 [1, 1152, 4608], P(None, 'fsdp')
- fc1_bias_grad: float32 [1, 4608], P(None, 'fsdp')
- fc2_weight_grad: float32 [1, 4608, 1152], P(None, 'fsdp')
- fc2_bias_grad: float32 [1, 1152], P(None, 'fsdp')
The draws below stay inside these ranges and needn't reach their ends.
All inputs are finite; a program needn't handle non-finite values.
Results may differ from the reference program's by a relative error of at most 0.019.
Values may be sent and summed in bfloat16 or wider, within the bound.
No kernel may reach another device: no remote copies, remote signals or barrier semaphores. Data moves between devices by JAX's collectives and lax.ppermute only.
A program may use at most 256 MiB of HBM per device.

```python
import jax
import jax.numpy as jnp
from jax import lax

D = 1152
HEADS = 16
FF = 4608
BLOCKS = 1
LENGTH = 512
IMAGES = 8


def draw_qkv_weight(key, part):
    full_shape = (BLOCKS, D, 3 * D)
    entries = jax.random.normal(key, full_shape, jnp.float32)
    return (jnp.clip(entries, -6.0, 6.0) * D ** (-0.5)).astype(jnp.bfloat16)


def steps_of(stream_key, extent, split, smallest, largest):
    loudness = 1.0
    for axis_at, shards_of in split:
        draws = jax.random.uniform(jax.random.fold_in(jax.random.fold_in(stream_key, 6), axis_at), (shards_of,), jnp.float32, smallest / len(split), largest / len(split))
        loudness = loudness * jnp.repeat(jnp.exp(draws), extent[axis_at] // shards_of).reshape((-1,) + (1,) * (len(extent) - 1 - axis_at))
    return loudness


def scatter_about(rng, dims, scale, most, split=(), held_as=jnp.bfloat16):
    level = steps_of(rng, dims, split, -0.22, 0.18) if split else 1.0
    values = jax.random.normal(rng, dims, jnp.float32) * scale * level
    return jnp.minimum(jnp.maximum(values, -most), most).astype(held_as)


def setup_inputs(seed: int = 0) -> dict:
    seeds = jax.random.split(jax.random.key(seed), 14)
    latents = scatter_about(seeds[0], (IMAGES, LENGTH, D), 1.0, 6.0, ((0, 8), (1, 4)))
    conditioning = scatter_about(seeds[1], (IMAGES, D), 1.0, 6.0, ((0, 8),), jnp.float32)
    modulation_weight = scatter_about(seeds[2], (BLOCKS, D, 6 * D), D ** -0.5, 0.1875, ((1, 8),))
    modulation_bias = scatter_about(seeds[3], (BLOCKS, 6 * D), 0.5, 3.0, ((1, 8),))
    qkv_weight = draw_qkv_weight(jax.random.fold_in(seeds[13], 71), 0)
    qkv_bias = scatter_about(seeds[5], (BLOCKS, 2 * D), 0.5, 3.0, ((1, 8),))
    proj_weight = scatter_about(seeds[6], (BLOCKS, D, D), (max(1, D // LENGTH)) ** -0.5, 4.0, ((1, 8),))
    proj_bias = scatter_about(seeds[7], (BLOCKS, D), 0.5, 3.0, ((1, 8),))
    fc1_weight = scatter_about(seeds[8], (BLOCKS, D, FF), D ** -0.5, 0.1875, ((1, 8),))
    fc1_bias = scatter_about(seeds[9], (BLOCKS, FF), 0.5, 3.0, ((1, 8),))
    fc2_weight = scatter_about(seeds[10], (BLOCKS, FF, D), FF ** -0.5, 0.09375, ((1, 8),))
    fc2_bias = scatter_about(seeds[11], (BLOCKS, D), 0.5, 3.0, ((1, 8),))
    cotangent = scatter_about(seeds[12], (IMAGES, LENGTH, D), 1.0, 6.0, ((0, 8), (1, 4)), jnp.float32)
    return dict(latents=latents, conditioning=conditioning, modulation_weight=modulation_weight, modulation_bias=modulation_bias, qkv_weight=qkv_weight, qkv_bias=qkv_bias, proj_weight=proj_weight, proj_bias=proj_bias, fc1_weight=fc1_weight, fc1_bias=fc1_bias, fc2_weight=fc2_weight, fc2_bias=fc2_bias, cotangent=cotangent)


NORM_EPS = 1e-06

def layer_norm(hidden):
    center = hidden - lax.optimization_barrier(jnp.mean(hidden, axis=-1, keepdims=True))
    inverse = lax.rsqrt(lax.optimization_barrier(jnp.mean(center * center, axis=-1, keepdims=True)) + NORM_EPS)
    return (center * inverse, inverse)

def norm_back(upstream, normed, inverse):
    return inverse * (upstream - lax.optimization_barrier(jnp.mean(upstream, axis=-1, keepdims=True)) - normed * lax.optimization_barrier(jnp.mean(upstream * normed, axis=-1, keepdims=True)))

def gelu_tanh(before):
    return jax.nn.gelu(before, approximate=True)

def to_heads(matrix):
    return matrix.reshape(matrix.shape[0], HEADS, D // HEADS).transpose(1, 0, 2)

def from_heads(stacked):
    return stacked.transpose(1, 0, 2).reshape(stacked.shape[1], D)

def head_forward(inputs):
    queries, key_rows, value_rows = inputs
    score_scale = (D // HEADS) ** (-0.5)
    scores = jnp.dot(queries, key_rows.T, preferred_element_type=jnp.float32) * score_scale
    row_peak = lax.optimization_barrier(jnp.max(scores, axis=-1, keepdims=True))
    log_total = jnp.log(lax.optimization_barrier(jnp.sum(jnp.exp(scores - row_peak), axis=-1, keepdims=True))) + row_peak
    probabilities = jnp.exp(scores - log_total).astype(jnp.bfloat16)
    mixture = jnp.dot(probabilities, value_rows, preferred_element_type=jnp.float32).astype(jnp.bfloat16)
    return (mixture, log_total[:, 0])

def head_backward(inputs):
    queries, key_rows, value_rows, mixture, log_total, upstream = inputs
    score_scale = (D // HEADS) ** (-0.5)
    scores = jnp.dot(queries, key_rows.T, preferred_element_type=jnp.float32) * score_scale
    probabilities = jnp.exp(scores - log_total[:, None])
    prob_low = probabilities.astype(jnp.bfloat16)
    d_probs = jnp.dot(upstream, value_rows.T, preferred_element_type=jnp.float32)
    delta = lax.optimization_barrier(jnp.sum(upstream.astype(jnp.float32) * mixture.astype(jnp.float32), axis=-1))
    d_scores = (probabilities * (d_probs - delta[:, None]) * score_scale).astype(jnp.bfloat16)
    d_queries = jnp.dot(d_scores, key_rows, preferred_element_type=jnp.float32).astype(jnp.bfloat16)
    d_keys = jnp.dot(d_scores.T, queries, preferred_element_type=jnp.float32).astype(jnp.bfloat16)
    d_values = jnp.dot(prob_low.T, upstream, preferred_element_type=jnp.float32).astype(jnp.bfloat16)
    return (d_queries, d_keys, d_values)

def block_forward(hidden, silu_cond, weights):
    modulation_weight, modulation_bias, qkv_weight, qkv_bias, proj_weight, proj_bias, fc1_weight, fc1_bias, fc2_weight, fc2_bias = weights
    feature_width = hidden.shape[-1]
    modulation = jnp.dot(silu_cond[None], modulation_weight, preferred_element_type=jnp.float32)[0]
    modulation = modulation + modulation_bias.astype(jnp.float32)
    pieces = [modulation[piece_index * feature_width:(piece_index + 1) * feature_width] for piece_index in range(6)]
    shift_attn, scale_attn, gate_attn, shift_mlp, scale_mlp, gate_mlp = pieces
    norm_attn, inv_attn = layer_norm(hidden)
    input_attn = (norm_attn * (1.0 + scale_attn) + shift_attn).astype(jnp.bfloat16)
    bias_row = qkv_bias.astype(jnp.float32)
    offsets = jnp.concatenate([bias_row[:feature_width], jnp.zeros((feature_width,), jnp.float32), bias_row[feature_width:]])
    packed = (jnp.dot(input_attn, qkv_weight, preferred_element_type=jnp.float32) + offsets).astype(jnp.bfloat16)
    queries = to_heads(packed[:, :feature_width])
    key_rows = to_heads(packed[:, feature_width:2 * feature_width])
    value_rows = to_heads(packed[:, 2 * feature_width:])
    mixture, log_totals = lax.map(head_forward, (queries, key_rows, value_rows))
    attended = from_heads(mixture)
    branch = jnp.dot(attended, proj_weight, preferred_element_type=jnp.float32) + proj_bias.astype(jnp.float32)
    middle = hidden + gate_attn * branch
    norm_mlp, inv_mlp = layer_norm(middle)
    input_mlp = (norm_mlp * (1.0 + scale_mlp) + shift_mlp).astype(jnp.bfloat16)
    before = jnp.dot(input_mlp, fc1_weight, preferred_element_type=jnp.float32) + fc1_bias.astype(jnp.float32)
    activated, pullback = jax.vjp(gelu_tanh, before)
    act_low = activated.astype(jnp.bfloat16)
    result = jnp.dot(act_low, fc2_weight, preferred_element_type=jnp.float32) + fc2_bias.astype(jnp.float32)
    output = middle + gate_mlp * result
    records = (pieces, norm_attn, inv_attn, input_attn, queries, key_rows, value_rows, mixture, log_totals, attended, branch, norm_mlp, inv_mlp, input_mlp, pullback, act_low, result)
    return (output, records)

def block_backward(upstream, records, silu_cond, weights):
    modulation_weight, modulation_bias, qkv_weight, qkv_bias, proj_weight, proj_bias, fc1_weight, fc1_bias, fc2_weight, fc2_bias = weights
    pieces, norm_attn, inv_attn, input_attn, queries, key_rows, value_rows, mixture, log_totals, attended, branch, norm_mlp, inv_mlp, input_mlp, pullback, act_low, result = records
    shift_attn, scale_attn, gate_attn, shift_mlp, scale_mlp, gate_mlp = pieces
    d_result = upstream * gate_mlp
    d_gate_mlp = lax.optimization_barrier(jnp.sum(upstream * result, axis=0))
    d_result_low = d_result.astype(jnp.bfloat16)
    fc2_weight_grad = jnp.dot(act_low.T, d_result_low, preferred_element_type=jnp.float32)
    fc2_bias_grad = lax.optimization_barrier(jnp.sum(d_result, axis=0))
    d_before = pullback(jnp.dot(d_result_low, fc2_weight.T, preferred_element_type=jnp.float32))[0]
    d_before_low = d_before.astype(jnp.bfloat16)
    fc1_weight_grad = jnp.dot(input_mlp.T, d_before_low, preferred_element_type=jnp.float32)
    fc1_bias_grad = lax.optimization_barrier(jnp.sum(d_before, axis=0))
    d_input_mlp = jnp.dot(d_before_low, fc1_weight.T, preferred_element_type=jnp.float32)
    d_scale_mlp = lax.optimization_barrier(jnp.sum(d_input_mlp * norm_mlp, axis=0))
    d_shift_mlp = lax.optimization_barrier(jnp.sum(d_input_mlp, axis=0))
    d_middle = upstream + norm_back(d_input_mlp * (1.0 + scale_mlp), norm_mlp, inv_mlp)
    d_branch = d_middle * gate_attn
    d_gate_attn = lax.optimization_barrier(jnp.sum(d_middle * branch, axis=0))
    d_branch_low = d_branch.astype(jnp.bfloat16)
    proj_weight_grad = jnp.dot(attended.T, d_branch_low, preferred_element_type=jnp.float32)
    proj_bias_grad = lax.optimization_barrier(jnp.sum(d_branch, axis=0))
    d_attended = jnp.dot(d_branch_low, proj_weight.T, preferred_element_type=jnp.float32).astype(jnp.bfloat16)
    d_queries, d_keys, d_values = lax.map(head_backward, (queries, key_rows, value_rows, mixture, log_totals, to_heads(d_attended)))
    query_grad = from_heads(d_queries)
    value_grad = from_heads(d_values)
    d_packed = jnp.concatenate([query_grad, from_heads(d_keys), value_grad], axis=-1)
    qkv_weight_grad = jnp.dot(input_attn.T, d_packed, preferred_element_type=jnp.float32)
    qkv_bias_grad = jnp.concatenate([lax.optimization_barrier(jnp.sum(query_grad.astype(jnp.float32), axis=0)), lax.optimization_barrier(jnp.sum(value_grad.astype(jnp.float32), axis=0))])
    d_input_attn = jnp.dot(d_packed, qkv_weight.T, preferred_element_type=jnp.float32)
    d_scale_attn = lax.optimization_barrier(jnp.sum(d_input_attn * norm_attn, axis=0))
    d_shift_attn = lax.optimization_barrier(jnp.sum(d_input_attn, axis=0))
    d_hidden = d_middle + norm_back(d_input_attn * (1.0 + scale_attn), norm_attn, inv_attn)
    d_modulation = jnp.concatenate([d_shift_attn, d_scale_attn, d_gate_attn, d_shift_mlp, d_scale_mlp, d_gate_mlp])
    silu_wide = silu_cond.astype(jnp.float32)
    modulation_weight_grad = silu_wide[:, None] * d_modulation[None, :]
    cond_part = lax.dot_general(d_modulation[None], modulation_weight.astype(jnp.float32), (((1,), (1,)), ((), ())), precision=lax.Precision.HIGHEST)[0]
    grads = (modulation_weight_grad, d_modulation, qkv_weight_grad, qkv_bias_grad, proj_weight_grad, proj_bias_grad, fc1_weight_grad, fc1_bias_grad, fc2_weight_grad, fc2_bias_grad)
    return (d_hidden, grads, cond_part)

def reference(latents, conditioning, modulation_weight, modulation_bias, qkv_weight, qkv_bias, proj_weight, proj_bias, fc1_weight, fc1_bias, fc2_weight, fc2_bias, cotangent):
    weights = (modulation_weight, modulation_bias, qkv_weight, qkv_bias, proj_weight, proj_bias, fc1_weight, fc1_bias, fc2_weight, fc2_bias)

    def one_image(totals, item):
        image, vector, upstream = item
        silu_cond = jax.nn.silu(vector).astype(jnp.bfloat16)
        hidden = image.astype(jnp.float32)
        record_list = []
        for section_index in range(BLOCKS):
            section_weights = tuple((weight[section_index] for weight in weights))
            hidden, records = block_forward(hidden, silu_cond, section_weights)
            record_list.append(records)
        output = hidden
        gradient = upstream.astype(jnp.float32)
        cond_sum = jnp.zeros(vector.shape, jnp.float32)
        for section_index in reversed(range(BLOCKS)):
            section_weights = tuple((weight[section_index] for weight in weights))
            gradient, grads, cond_part = block_backward(gradient, record_list[section_index], silu_cond, section_weights)
            totals = tuple((total_sum.at[section_index].add(grad_piece) for total_sum, grad_piece in zip(totals, grads)))
            cond_sum = cond_sum + cond_part
        silu_pull = jax.vjp(jax.nn.silu, vector)[1]
        return (totals, (output, gradient, silu_pull(cond_sum)[0]))
    initial = tuple((jnp.zeros(weight.shape, jnp.float32) for weight in weights))
    totals, outputs = lax.scan(one_image, initial, (latents, conditioning, cotangent))
    block_output, latents_grad, conditioning_grad = outputs
    modulation_weight_grad, modulation_bias_grad, qkv_weight_grad, qkv_bias_grad, proj_weight_grad, proj_bias_grad, fc1_weight_grad, fc1_bias_grad, fc2_weight_grad, fc2_bias_grad = totals
    return (block_output, latents_grad, conditioning_grad, modulation_weight_grad, modulation_bias_grad, qkv_weight_grad, qkv_bias_grad, proj_weight_grad, proj_bias_grad, fc1_weight_grad, fc1_bias_grad, fc2_weight_grad, fc2_bias_grad)
```

```python
import jax
import jax.numpy as jnp
from jax import lax
from jax.experimental import pallas as pl
from jax.experimental.pallas import tpu as pltpu
from jax.sharding import PartitionSpec as P


HEADS = 16
NORM_EPS = 1e-06


def layer_norm(hidden):
    center = hidden - jnp.mean(hidden, axis=-1, keepdims=True)
    inverse = lax.rsqrt(jnp.mean(center * center, axis=-1, keepdims=True) + NORM_EPS)
    return (center * inverse, inverse)


def norm_back(upstream, normed, inverse):
    return inverse * (
        upstream
        - jnp.mean(upstream, axis=-1, keepdims=True)
        - normed * jnp.mean(upstream * normed, axis=-1, keepdims=True)
    )


def gelu_tanh(before):
    return jax.nn.gelu(before, approximate=True)


def dot(left, right):
    return jnp.dot(left, right, preferred_element_type=jnp.float32)


def dot_back(left, weight):
    return lax.dot_general(
        left, weight, (((left.ndim - 1,), (1,)), ((), ())), preferred_element_type=jnp.float32
    )


def dot_rows(left, right):
    return lax.dot_general(left, right, (((0,), (0,)), ((), ())), preferred_element_type=jnp.float32)


def swap(value, axis, mask):
    pairs = [(i, i ^ mask) for i in range(lax.axis_size(axis))]
    return lax.ppermute(value, axis, pairs)


def bits_of(size):
    bits = []
    step = 1
    while step < size:
        bits.append(step)
        step *= 2
    return bits


def seq_gather(value):
    near = swap(value, "seq", 1)
    far = swap(value, "seq", 2)
    both = swap(far, "seq", 1)
    return jnp.concatenate([value, near, far, both], axis=0)


def seq_blocks(block):
    low = block.astype(jnp.bfloat16)
    return seq_gather(low).reshape((-1,) + low.shape)


def seq_exchange(blocks):
    if blocks.shape[0] == 1:
        return blocks
    pairs = blocks.reshape((-1, 2) + blocks.shape[1:])
    near = swap(pairs[:, 1], "seq", 1)
    kept = jnp.stack([pairs[:, 0], near], axis=1)
    far = swap(kept[1], "seq", 2)
    return jnp.concatenate([kept[0], far], axis=0)


def seq_reduce(partial):
    size = lax.axis_size("seq")
    rows = partial.shape[0] // size
    for mask in bits_of(size):
        count = partial.shape[0] // rows
        blocks = partial.reshape((count // 2, 2) + (rows,) + partial.shape[1:])
        kept, sent = blocks[:, 0], blocks[:, 1]
        received = swap(sent.astype(jnp.bfloat16), "seq", mask)
        partial = (kept + received.astype(jnp.float32)).reshape((-1,) + partial.shape[1:])
    return partial


def tie(*values):
    return lax.optimization_barrier(values)


def reduce_near(partial):
    size = lax.axis_size("fsdp")
    near = lax.axis_index("fsdp") % 2
    rows = partial.shape[0] // size
    blocks = partial.astype(jnp.bfloat16).reshape((size // 2, 2, rows) + partial.shape[1:])
    kept = lax.dynamic_index_in_dim(blocks, near, 1, keepdims=False)
    sent = lax.dynamic_index_in_dim(blocks, 1 - near, 1, keepdims=False)
    return (kept, swap(sent, "fsdp", 1))


def reduce_far(kept, received):
    far = lax.axis_index("fsdp") // 2
    pair = kept.astype(jnp.float32) + received.astype(jnp.float32)
    total = lax.dynamic_index_in_dim(pair, far, 0, keepdims=False)
    low = pair.astype(jnp.bfloat16)
    for k in range(1, pair.shape[0]):
        piece = lax.dynamic_index_in_dim(low, far ^ k, 0, keepdims=False)
        total = total + swap(piece, "fsdp", 2 * k).astype(jnp.float32)
    return total


def lanes(columns):
    return -(-columns // 128) * 128


def in_vmem(count):
    return [pl.BlockSpec(memory_space=pltpu.VMEM) for _ in range(count)]


def own_columns_of(whole, part, groups, parts):
    span = whole.shape[1] // (groups * parts)
    starts = [(group * parts + part) * span for group in range(groups)]
    return [whole[:, start : start + span] for start in starts]


def take_attention(qkv, proj, index, parts):
    rows = qkv.shape[0]
    used = qkv.shape[1] // parts
    columns = lanes(used) + proj.shape[1] // parts

    def kernel(at_ref, qkv_ref, proj_ref, target):
        for part in range(parts):

            @pl.when(at_ref[0] == part)
            def _():
                pieces = own_columns_of(qkv_ref[...], part, 3, parts)
                pieces.append(jnp.zeros((rows, lanes(used) - used), qkv.dtype))
                pieces += own_columns_of(proj_ref[...], part, 1, parts)
                target[...] = jnp.concatenate(pieces, axis=1)

    return pl.pallas_call(
        kernel,
        out_shape=jax.ShapeDtypeStruct((rows, columns), qkv.dtype),
        in_specs=[pl.BlockSpec(memory_space=pltpu.SMEM)] + in_vmem(2),
        out_specs=in_vmem(1)[0],
        name="take_attention",
    )(index.reshape(1), qkv, proj)


def take_feed_forward(fc1, fc2, index, groups, parts):
    rows, width = fc1.shape[0], fc2.shape[1]
    quarter = fc2.shape[0] // parts

    def kernel(at_ref, fc1_ref, fc2_ref, target):
        for part in range(parts):

            @pl.when(at_ref[0] == part)
            def _():
                pieces = own_columns_of(fc1_ref[...], part, groups, parts)
                target[0] = jnp.concatenate(pieces, axis=1)
                target[1] = fc2_ref[part * quarter : (part + 1) * quarter]

    return pl.pallas_call(
        kernel,
        out_shape=jax.ShapeDtypeStruct((2, rows, width), fc1.dtype),
        in_specs=[pl.BlockSpec(memory_space=pltpu.SMEM)] + in_vmem(2),
        out_specs=in_vmem(1)[0],
        name="take_feed_forward",
    )(index.reshape(1), fc1, fc2)


def pack_near(grad, blocks, index, near, devices):
    group = blocks.shape[1]
    rows, used = grad.shape[0] // devices, grad.shape[1]
    shape = (devices // 2, rows, used + blocks.shape[2])

    def kernel(at_ref, grad_ref, blocks_ref, kept_ref, sent_ref):
        for side in range(2):

            @pl.when(at_ref[1] == side)
            def _():
                for owner in range(devices):
                    target = kept_ref if owner % 2 == side else sent_ref
                    part, start = divmod(owner * rows, group)
                    target[owner // 2, :, :used] = grad_ref[owner * rows : (owner + 1) * rows]
                    target[owner // 2, :, used:] = blocks_ref[at_ref[0] ^ part][start : start + rows]

    return pl.pallas_call(
        kernel,
        out_shape=[jax.ShapeDtypeStruct(shape, grad.dtype)] * 2,
        in_specs=[pl.BlockSpec(memory_space=pltpu.SMEM)] + in_vmem(2),
        out_specs=in_vmem(2),
        name="pack_near",
    )(jnp.stack([index, near]), grad, blocks)


def split_columns(whole, index, parts):
    rows, columns = whole.shape
    span = columns // parts

    def kernel(at_ref, source, target):
        for own in range(parts):

            @pl.when(at_ref[0] == own)
            def _():
                values = source[...]
                for part in range(parts):
                    start = (own ^ part) * span
                    target[part] = values[:, start : start + span]

    return pl.pallas_call(
        kernel,
        out_shape=jax.ShapeDtypeStruct((parts, rows, span), whole.dtype),
        in_specs=[pl.BlockSpec(memory_space=pltpu.SMEM)] + in_vmem(1),
        out_specs=in_vmem(1)[0],
        name="split_columns",
    )(index.reshape(1), whole)


def join_columns(blocks, index, groups, dtype):
    parts, rows, columns = blocks.shape
    span = columns // groups

    def kernel(at_ref, source, target):
        own = at_ref[0]
        wholes = [source[own ^ part].astype(dtype) for part in range(parts)]
        pieces = []
        for group in range(groups):
            for part in range(parts):
                pieces.append(wholes[part][:, group * span : (group + 1) * span])
        target[...] = jnp.concatenate(pieces, axis=1)

    return pl.pallas_call(
        kernel,
        out_shape=jax.ShapeDtypeStruct((rows, parts * columns), dtype),
        in_specs=[pl.BlockSpec(memory_space=pltpu.SMEM)] + in_vmem(1),
        out_specs=in_vmem(1)[0],
        name="join_columns",
    )(index.reshape(1), blocks)


def join_attention(blocks, index, span):
    parts, rows, columns = blocks.shape
    starts = [0, span, 2 * span, columns - span]

    def kernel(at_ref, source, qkv_ref, proj_ref):
        own = at_ref[0]
        wholes = [source[own ^ part].astype(jnp.float32) for part in range(parts)]
        pieces = []
        for start in starts:
            for part in range(parts):
                pieces.append(wholes[part][:, start : start + span])
        qkv_ref[...] = jnp.concatenate(pieces[: 3 * parts], axis=1)
        proj_ref[...] = jnp.concatenate(pieces[3 * parts :], axis=1)

    return pl.pallas_call(
        kernel,
        out_shape=[
            jax.ShapeDtypeStruct((rows, 3 * parts * span), jnp.float32),
            jax.ShapeDtypeStruct((rows, parts * span), jnp.float32),
        ],
        in_specs=[pl.BlockSpec(memory_space=pltpu.SMEM)] + in_vmem(1),
        out_specs=in_vmem(2),
        name="join_attention",
    )(index.reshape(1), blocks)


def join_rows(blocks, index, dtype):
    parts, rows, columns = blocks.shape

    def kernel(at_ref, source, target):
        for part in range(parts):
            target[part * rows : (part + 1) * rows] = source[at_ref[0] ^ part].astype(dtype)

    return pl.pallas_call(
        kernel,
        out_shape=jax.ShapeDtypeStruct((parts * rows, columns), dtype),
        in_specs=[pl.BlockSpec(memory_space=pltpu.SMEM)] + in_vmem(1),
        out_specs=in_vmem(1)[0],
        name="join_rows",
    )(index.reshape(1), blocks)


def small_gather(row, axis):
    own = lax.axis_index(axis)
    rows = row
    for mask in bits_of(lax.axis_size(axis)):
        other = swap(rows, axis, mask)
        upper = (own & mask) != 0
        rows = jnp.concatenate(
            [jnp.where(upper, other, rows), jnp.where(upper, rows, other)], axis=0
        )
    return rows


def small_reduce(rows, axis):
    own = lax.axis_index(axis)
    for mask in reversed(bits_of(lax.axis_size(axis))):
        half = rows.shape[0] // 2
        upper = (own & mask) != 0
        kept = jnp.where(upper, rows[half:], rows[:half])
        sent = jnp.where(upper, rows[:half], rows[half:])
        rows = kept + swap(sent, axis, mask)
    return rows


def seq_sum(value):
    for mask in bits_of(lax.axis_size("seq")):
        value = value + swap(value, "seq", mask)
    return value


def shards(
    latents,
    conditioning,
    modulation_weight,
    modulation_bias,
    qkv_weight,
    qkv_bias,
    proj_weight,
    proj_bias,
    fc1_weight,
    fc1_bias,
    fc2_weight,
    fc2_bias,
    cotangent,
):
    f32, bf16 = jnp.float32, jnp.bfloat16
    seq, fsdp = lax.axis_size("seq"), lax.axis_size("fsdp")
    s, f = lax.axis_index("seq"), lax.axis_index("fsdp")
    hidden = latents[0].astype(f32)
    upstream = cotangent[0]
    width = hidden.shape[1]
    group = width // seq
    head_width = width // HEADS
    local_heads = HEADS // seq
    rows = qkv_weight.shape[1]
    unit_rows = fc2_weight.shape[1]
    quarter = unit_rows // seq
    units = quarter * fsdp
    score_scale = head_width ** (-0.5)

    silu_cond = jax.nn.silu(conditioning).astype(bf16)
    shorts = [silu_cond, qkv_bias, proj_bias, fc1_bias, fc2_bias]
    gathered = small_gather(jnp.concatenate(shorts, axis=1), "fsdp")
    split = []
    at = 0
    for short in shorts:
        split.append(gathered[:, at : at + short.shape[1]])
        at += short.shape[1]
    silu_all = split[0]
    qkv_offset, proj_offset, fc1_offset, fc2_offset = [
        part.astype(f32).reshape(1, -1) for part in split[1:]
    ]

    attention_own = take_attention(qkv_weight[0], proj_weight[0], s, seq)
    attention_full = lax.all_gather(attention_own, "fsdp", axis=0, tiled=True)
    padded = lanes(3 * group)
    qkv_full = attention_full[:, :padded]
    proj_blocks = attention_full[:, padded:].reshape(seq, group, group)
    proj_blocks = jnp.stack(
        [lax.dynamic_index_in_dim(proj_blocks, s ^ k, 0, keepdims=False) for k in range(seq)]
    )
    proj_full = join_columns(seq_exchange(proj_blocks), s, 1, bf16)
    forward_own = take_feed_forward(fc1_weight[0], fc2_weight[0], s, fsdp, seq)

    silu_own = lax.dynamic_slice_in_dim(silu_all, f * rows, rows, 1)
    partial = dot(silu_own, modulation_weight[0])
    bias_row = lax.dynamic_update_slice_in_dim(
        jnp.zeros((1, 6 * width), f32),
        modulation_bias.astype(f32),
        f * modulation_bias.shape[1],
        1,
    )
    modulation = small_reduce(partial + bias_row, "fsdp")
    shift_attn, scale_attn, gate_attn, shift_mlp, scale_mlp, gate_mlp = [
        modulation[:, at * width : (at + 1) * width] for at in range(6)
    ]

    norm_attn, inv_attn = layer_norm(hidden)
    low_attn = (norm_attn * (1.0 + scale_attn) + shift_attn).astype(bf16)
    low_attn, forward_own = tie(low_attn, forward_own)
    input_attn = seq_gather(low_attn)
    forward_full = lax.all_gather(forward_own, "fsdp", axis=1, tiled=True)
    fc1_full, fc2_full = forward_full[0], forward_full[1]
    d_result = upstream * gate_mlp
    low_result, packed_weight = tie(d_result.astype(bf16), qkv_full)
    d_result_low = seq_gather(low_result)

    query_bias = lax.dynamic_slice_in_dim(qkv_offset[:, :width], s * group, group, 1)
    value_bias = lax.dynamic_slice_in_dim(qkv_offset[:, width:], s * group, group, 1)
    zeros = jnp.zeros((1, group), f32)
    offsets = jnp.concatenate(
        [query_bias, zeros, value_bias, zeros[:, : padded - 3 * group]], axis=1
    )
    packed = (dot(input_attn, packed_weight) + offsets).astype(bf16)
    length = packed.shape[0]
    heads = packed[:, : 3 * group].reshape(length, 3, local_heads, head_width)
    queries, key_rows, value_rows = heads[:, 0], heads[:, 1], heads[:, 2]
    scores = (
        jnp.einsum("qhd,khd->hqk", queries, key_rows, preferred_element_type=f32) * score_scale
    )
    row_peak = jnp.max(scores, axis=-1, keepdims=True)
    log_total = jnp.log(jnp.sum(jnp.exp(scores - row_peak), axis=-1, keepdims=True)) + row_peak
    probabilities = jnp.exp(scores - log_total)
    prob_low = probabilities.astype(bf16)
    attended = jnp.einsum("hqk,khd->qhd", prob_low, value_rows, preferred_element_type=f32).astype(
        bf16
    )
    attended_flat = attended.reshape(length, group)
    branch_part = dot(attended_flat, proj_full)
    branch = seq_reduce(branch_part) + proj_offset
    middle = hidden + gate_attn * branch

    norm_mlp, inv_mlp = layer_norm(middle)
    low_mlp = (norm_mlp * (1.0 + scale_mlp) + shift_mlp).astype(bf16)
    low_mlp, d_result_low = tie(low_mlp, d_result_low)
    input_mlp = seq_gather(low_mlp)
    fc1_offset_own = lax.dynamic_index_in_dim(
        fc1_offset.reshape(fsdp, seq, quarter), s, 1, keepdims=False
    ).reshape(1, units)
    before = dot(input_mlp, fc1_full) + fc1_offset_own
    activated, pullback = jax.vjp(gelu_tanh, before)
    act_low = activated.astype(bf16)
    d_before = pullback(dot_back(d_result_low, fc2_full))[0]
    d_before_low = d_before.astype(bf16)
    fc2_near = reduce_near(dot_rows(act_low, d_result_low))
    d_input_part = dot_back(d_before_low, fc1_full)
    fc1_near = reduce_near(dot_rows(input_mlp, d_before_low))
    d_input_part, act_late = tie(d_input_part, act_low)
    d_input_mlp = seq_reduce(d_input_part)
    result = seq_reduce(dot(act_late, fc2_full)) + fc2_offset
    output = middle + gate_mlp * result
    d_gate_mlp = jnp.sum(upstream * result, axis=0, keepdims=True)
    fc2_bias_part = jnp.sum(d_result, axis=0, keepdims=True)
    fc1_bias_part = jnp.sum(d_before, axis=0, keepdims=True)
    d_scale_mlp = jnp.sum(d_input_mlp * norm_mlp, axis=0, keepdims=True)
    d_shift_mlp = jnp.sum(d_input_mlp, axis=0, keepdims=True)
    d_middle = upstream + norm_back(d_input_mlp * (1.0 + scale_mlp), norm_mlp, inv_mlp)

    d_branch = d_middle * gate_attn
    d_gate_attn = jnp.sum(d_middle * branch, axis=0, keepdims=True)
    proj_bias_part = jnp.sum(d_branch, axis=0, keepdims=True)
    low_branch = d_branch.astype(bf16)
    d_branch_low = seq_gather(low_branch)
    fc2_grad = reduce_far(*fc2_near)
    proj_grad = split_columns(dot_rows(attended_flat, d_branch_low).astype(bf16), s, seq)
    proj_grad, d_branch_low = tie(proj_grad, d_branch_low)
    proj_grad = seq_exchange(proj_grad)
    d_attended = dot_back(d_branch_low, proj_full).astype(bf16).reshape(attended.shape)
    d_probs = jnp.einsum("qhd,khd->hqk", d_attended, value_rows, preferred_element_type=f32)
    delta = jnp.sum(d_attended.astype(f32) * attended.astype(f32), axis=-1).T
    d_scores = (probabilities * (d_probs - delta[..., None]) * score_scale).astype(bf16)
    d_queries = jnp.einsum("hqk,khd->qhd", d_scores, key_rows, preferred_element_type=f32)
    d_keys = jnp.einsum("hqk,qhd->khd", d_scores, queries, preferred_element_type=f32)
    d_values = jnp.einsum("hqk,qhd->khd", prob_low, d_attended, preferred_element_type=f32)
    d_packed = jnp.concatenate(
        [grad.astype(bf16).reshape(length, group) for grad in (d_queries, d_keys, d_values)]
        + [jnp.zeros((length, padded - 3 * group), bf16)],
        axis=1,
    )
    d_input_part = dot_back(d_packed, qkv_full)
    d_input_attn = seq_reduce(d_input_part)
    fc1_grad = reduce_far(*fc1_near)
    qkv_grad = dot_rows(input_attn, d_packed).astype(bf16)
    kept, sent = pack_near(qkv_grad, proj_grad, s, f % 2, fsdp)
    attention_near = (kept, swap(sent, "fsdp", 1))
    qkv_sum = jnp.sum(d_packed.astype(f32), axis=0, keepdims=True)
    d_scale_attn = jnp.sum(d_input_attn * norm_attn, axis=0, keepdims=True)
    d_shift_attn = jnp.sum(d_input_attn, axis=0, keepdims=True)
    latents_grad = d_middle + norm_back(d_input_attn * (1.0 + scale_attn), norm_attn, inv_attn)

    sums = seq_sum(
        jnp.concatenate(
            [
                d_shift_attn,
                d_scale_attn,
                d_gate_attn,
                d_shift_mlp,
                d_scale_mlp,
                d_gate_mlp,
                proj_bias_part,
                fc2_bias_part,
            ],
            axis=1,
        )
    )
    own_columns = jnp.concatenate(
        [qkv_sum[:, :group], qkv_sum[:, 2 * group : 3 * group], fc1_bias_part], axis=1
    )
    columns = small_gather(own_columns, "seq")
    query_sum = columns[:, :group].reshape(1, -1)
    value_sum = columns[:, group : 2 * group].reshape(1, -1)
    fc1_sum = jnp.moveaxis(columns[:, 2 * group :].reshape(seq, fsdp, quarter), 0, 1).reshape(1, -1)
    every = small_gather(
        jnp.concatenate([sums, query_sum, value_sum, fc1_sum], axis=1), "fsdp"
    )
    every, kept, received = tie(every, *attention_near)
    d_modulation = every[:, : 6 * width]
    weight_grad = lax.dot_general(
        silu_own.astype(f32),
        d_modulation,
        (((0,), (0,)), ((), ())),
        precision=lax.Precision.HIGHEST,
    )
    totals = jnp.sum(every, axis=0, keepdims=True)

    def own_part(start, count):
        part = count // fsdp
        return lax.dynamic_slice_in_dim(totals[:, start : start + count], f * part, part, 1)

    modulation_bias_grad = own_part(0, 6 * width)
    proj_bias_grad = own_part(6 * width, width)
    fc2_bias_grad = own_part(7 * width, width)
    qkv_bias_grad = own_part(8 * width, 2 * width)
    fc1_bias_grad = own_part(10 * width, fc1_offset.shape[1])

    cond_rows = lax.dot_general(
        d_modulation,
        modulation_weight[0].astype(f32),
        (((1,), (1,)), ((), ())),
        precision=lax.Precision.HIGHEST,
    )
    cond_all = small_gather(cond_rows.reshape(1, -1), "fsdp").reshape(fsdp, fsdp, rows)
    cond_sum = lax.dynamic_index_in_dim(cond_all, f, 1, keepdims=False).reshape(1, width)
    conditioning_grad = jax.vjp(jax.nn.silu, conditioning)[1](cond_sum)[0]

    fc2_out = join_rows(seq_blocks(fc2_grad), s, f32)
    fc1_out = join_columns(seq_blocks(fc1_grad), s, fsdp, f32)
    attention_grad = reduce_far(kept, received)
    qkv_out, proj_out = join_attention(seq_blocks(attention_grad), s, group)
    return (
        output[None],
        latents_grad[None],
        conditioning_grad,
        weight_grad[None],
        modulation_bias_grad,
        qkv_out[None],
        qkv_bias_grad,
        proj_out[None],
        proj_bias_grad,
        fc1_out[None],
        fc1_bias_grad,
        fc2_out[None],
        fc2_bias_grad,
    )


def solution(mesh):
    tokens = P("fsdp", "seq", None)
    matrix = P(None, "fsdp", None)
    vector = P(None, "fsdp")
    cond = P("fsdp", None)
    weights = (matrix, vector) * 5

    return jax.shard_map(
        shards,
        mesh=mesh,
        in_specs=(tokens, cond) + weights + (tokens,),
        out_specs=(tokens, tokens, cond) + weights,
        check_vma=False,
    )
```

```python
import jax
import jax.numpy as jnp
from jax import lax
from jax.experimental import pallas as pl
from jax.experimental.pallas import tpu as pltpu
from jax.sharding import PartitionSpec as P


HEADS = 16
NORM_EPS = 1e-06


def layer_norm(hidden):
    center = hidden - jnp.mean(hidden, axis=-1, keepdims=True)
    inverse = lax.rsqrt(jnp.mean(center * center, axis=-1, keepdims=True) + NORM_EPS)
    return (center * inverse, inverse)


def norm_back(upstream, normed, inverse):
    return inverse * (
        upstream
        - jnp.mean(upstream, axis=-1, keepdims=True)
        - normed * jnp.mean(upstream * normed, axis=-1, keepdims=True)
    )


def gelu_tanh(before):
    return jax.nn.gelu(before, approximate=True)


def dot(left, right):
    return jnp.dot(left, right, preferred_element_type=jnp.float32)


def dot_back(left, weight):
    return lax.dot_general(
        left, weight, (((left.ndim - 1,), (1,)), ((), ())), preferred_element_type=jnp.float32
    )


def dot_rows(left, right):
    return lax.dot_general(left, right, (((0,), (0,)), ((), ())), preferred_element_type=jnp.float32)


def swap(value, axis, mask):
    pairs = [(i, i ^ mask) for i in range(lax.axis_size(axis))]
    return lax.ppermute(value, axis, pairs)


def bits_of(size):
    bits = []
    step = 1
    while step < size:
        bits.append(step)
        step *= 2
    return bits


def seq_gather(value):
    return jnp.concatenate(seq_blocks(value), axis=0)


def seq_blocks(value):
    blocks = {0: value}
    for mask in reversed(bits_of(lax.axis_size("seq"))):
        for tag in list(blocks):
            blocks[tag ^ mask] = swap(blocks[tag], "seq", mask)
    return [blocks[tag] for tag in range(len(blocks))]


def seq_exchange(blocks):
    count = len(blocks)
    blocks = list(blocks)
    for mask in bits_of(count):
        kept = [tag for tag in range(count) if not tag & mask]
        received = swap(jnp.stack([blocks[tag | mask] for tag in kept]), "seq", mask)
        moved = {tag | mask: received[at] for at, tag in enumerate(kept)}
        blocks = [moved.get(tag, blocks[tag]) for tag in range(count)]
    return blocks


def seq_reduce(partial):
    size = lax.axis_size("seq")
    rows = partial.shape[0] // size
    for mask in bits_of(size):
        count = partial.shape[0] // rows
        blocks = partial.reshape((count // 2, 2) + (rows,) + partial.shape[1:])
        kept, sent = blocks[:, 0], blocks[:, 1]
        received = swap(sent.astype(jnp.bfloat16), "seq", mask)
        partial = (kept + received.astype(jnp.float32)).reshape((-1,) + partial.shape[1:])
    return partial


def tie(*values):
    return lax.optimization_barrier(values)


def reduce_near(partial):
    size = lax.axis_size("fsdp")
    near = lax.axis_index("fsdp") % 2
    rows = partial.shape[0] // size
    blocks = partial.astype(jnp.bfloat16).reshape((size // 2, 2, rows) + partial.shape[1:])
    kept = lax.dynamic_index_in_dim(blocks, near, 1, keepdims=False)
    sent = lax.dynamic_index_in_dim(blocks, 1 - near, 1, keepdims=False)
    return (kept, swap(sent, "fsdp", 1))


def reduce_far(kept, received):
    far = lax.axis_index("fsdp") // 2
    pair = kept.astype(jnp.float32) + received.astype(jnp.float32)
    total = lax.dynamic_index_in_dim(pair, far, 0, keepdims=False)
    low = pair.astype(jnp.bfloat16)
    for k in range(1, pair.shape[0]):
        piece = lax.dynamic_index_in_dim(low, far ^ k, 0, keepdims=False)
        total = total + swap(piece, "fsdp", 2 * k).astype(jnp.float32)
    return total


def lanes(columns):
    return -(-columns // 128) * 128


def in_vmem(count):
    return [pl.BlockSpec(memory_space=pltpu.VMEM) for _ in range(count)]


def own_columns_of(whole, part, groups, parts):
    span = whole.shape[1] // (groups * parts)
    starts = [(group * parts + part) * span for group in range(groups)]
    return [whole[:, start : start + span] for start in starts]


def take_attention(qkv, proj, index, parts):
    rows = qkv.shape[0]
    used = qkv.shape[1] // parts
    columns = lanes(used) + proj.shape[1] // parts

    def kernel(at_ref, qkv_ref, proj_ref, target):
        for part in range(parts):

            @pl.when(at_ref[0] == part)
            def _():
                pieces = own_columns_of(qkv_ref[...], part, 3, parts)
                pieces.append(jnp.zeros((rows, lanes(used) - used), qkv.dtype))
                pieces += own_columns_of(proj_ref[...], part, 1, parts)
                target[...] = jnp.concatenate(pieces, axis=1)

    return pl.pallas_call(
        kernel,
        out_shape=jax.ShapeDtypeStruct((rows, columns), qkv.dtype),
        in_specs=[pl.BlockSpec(memory_space=pltpu.SMEM)] + in_vmem(2),
        out_specs=in_vmem(1)[0],
        name="take_attention",
    )(index.reshape(1), qkv, proj)


def take_feed_forward(fc1, fc2, index, groups, parts):
    rows, width = fc1.shape[0], fc2.shape[1]
    quarter = fc2.shape[0] // parts

    def kernel(at_ref, fc1_ref, fc2_ref, target):
        for part in range(parts):

            @pl.when(at_ref[0] == part)
            def _():
                pieces = own_columns_of(fc1_ref[...], part, groups, parts)
                target[0] = jnp.concatenate(pieces, axis=1)
                target[1] = fc2_ref[part * quarter : (part + 1) * quarter]

    return pl.pallas_call(
        kernel,
        out_shape=jax.ShapeDtypeStruct((2, rows, width), fc1.dtype),
        in_specs=[pl.BlockSpec(memory_space=pltpu.SMEM)] + in_vmem(2),
        out_specs=in_vmem(1)[0],
        name="take_feed_forward",
    )(index.reshape(1), fc1, fc2)


def pick(refs, index, dtype):
    value = refs[0][...]
    for at in range(1, len(refs)):
        value = jnp.where(index == at, refs[at][...], value)
    return value.astype(dtype)


def split_columns(whole, index, parts):
    rows, columns = whole.shape
    span = columns // parts

    def kernel(at_ref, source, target):
        for own in range(parts):

            @pl.when(at_ref[0] == own)
            def _():
                values = source[...]
                for part in range(parts):
                    start = (own ^ part) * span
                    target[part] = values[:, start : start + span]

    return pl.pallas_call(
        kernel,
        out_shape=jax.ShapeDtypeStruct((parts, rows, span), whole.dtype),
        in_specs=[pl.BlockSpec(memory_space=pltpu.SMEM)] + in_vmem(1),
        out_specs=in_vmem(1)[0],
        name="split_columns",
    )(index.reshape(1), whole)


def join_columns(blocks, index, groups, span, dtype):
    parts, rows = len(blocks), blocks[0].shape[0]

    def kernel(at_ref, *refs):
        target = refs[-1]
        wholes = [pick(refs[:-1], at_ref[0] ^ part, dtype) for part in range(parts)]
        pieces = []
        for group in range(groups):
            for part in range(parts):
                pieces.append(wholes[part][:, group * span : (group + 1) * span])
        target[...] = jnp.concatenate(pieces, axis=1)

    return pl.pallas_call(
        kernel,
        out_shape=jax.ShapeDtypeStruct((rows, parts * groups * span), dtype),
        in_specs=[pl.BlockSpec(memory_space=pltpu.SMEM)] + in_vmem(parts),
        out_specs=in_vmem(1)[0],
        name="join_columns",
    )(index.reshape(1), *blocks)


def join_rows(blocks, index, dtype):
    parts = len(blocks)
    rows, columns = blocks[0].shape

    def kernel(at_ref, *refs):
        target = refs[-1]
        for part in range(parts):
            value = pick(refs[:-1], at_ref[0] ^ part, dtype)
            target[part * rows : (part + 1) * rows] = value

    return pl.pallas_call(
        kernel,
        out_shape=jax.ShapeDtypeStruct((parts * rows, columns), dtype),
        in_specs=[pl.BlockSpec(memory_space=pltpu.SMEM)] + in_vmem(parts),
        out_specs=in_vmem(1)[0],
        name="join_rows",
    )(index.reshape(1), *blocks)


def small_gather(row, axis):
    own = lax.axis_index(axis)
    rows = row
    for mask in bits_of(lax.axis_size(axis)):
        other = swap(rows, axis, mask)
        upper = (own & mask) != 0
        rows = jnp.concatenate(
            [jnp.where(upper, other, rows), jnp.where(upper, rows, other)], axis=0
        )
    return rows


def small_reduce(rows, axis):
    own = lax.axis_index(axis)
    for mask in bits_of(lax.axis_size(axis)):
        pairs = rows.reshape(rows.shape[0] // 2, 2, rows.shape[1])
        upper = (own & mask) != 0
        kept = jnp.where(upper, pairs[:, 1], pairs[:, 0])
        sent = jnp.where(upper, pairs[:, 0], pairs[:, 1])
        rows = kept + swap(sent, axis, mask)
    return rows


def seq_sum(value):
    for mask in bits_of(lax.axis_size("seq")):
        value = value + swap(value, "seq", mask)
    return value


def shards(
    latents,
    conditioning,
    modulation_weight,
    modulation_bias,
    qkv_weight,
    qkv_bias,
    proj_weight,
    proj_bias,
    fc1_weight,
    fc1_bias,
    fc2_weight,
    fc2_bias,
    cotangent,
):
    f32, bf16 = jnp.float32, jnp.bfloat16
    seq, fsdp = lax.axis_size("seq"), lax.axis_size("fsdp")
    s, f = lax.axis_index("seq"), lax.axis_index("fsdp")
    hidden = latents[0].astype(f32)
    upstream = cotangent[0]
    width = hidden.shape[1]
    group = width // seq
    head_width = width // HEADS
    local_heads = HEADS // seq
    rows = qkv_weight.shape[1]
    unit_rows = fc2_weight.shape[1]
    quarter = unit_rows // seq
    units = quarter * fsdp
    score_scale = head_width ** (-0.5)

    attention_own = take_attention(qkv_weight[0], proj_weight[0], s, seq)
    attention_own, vector = tie(attention_own, conditioning)
    silu_cond = jax.nn.silu(vector).astype(bf16)
    shorts = [silu_cond, qkv_bias, proj_bias, fc1_bias, fc2_bias]
    gathered = small_gather(jnp.concatenate(shorts, axis=1), "fsdp")
    split = []
    at = 0
    for short in shorts:
        split.append(gathered[:, at : at + short.shape[1]])
        at += short.shape[1]
    silu_all = split[0]
    qkv_offset, proj_offset, fc1_offset, fc2_offset = [
        part.astype(f32).reshape(1, -1) for part in split[1:]
    ]

    attention_full = lax.all_gather(attention_own, "fsdp", axis=0, tiled=True)
    padded = lanes(3 * group)
    qkv_full = attention_full[:, :padded]
    proj_blocks = attention_full[:, padded:].reshape(seq, group, group)
    proj_blocks = [
        lax.dynamic_index_in_dim(proj_blocks, s ^ k, 0, keepdims=False) for k in range(seq)
    ]
    proj_full = join_columns(seq_exchange(proj_blocks), s, 1, group, bf16)
    forward_own = take_feed_forward(fc1_weight[0], fc2_weight[0], s, fsdp, seq)

    silu_own = lax.dynamic_slice_in_dim(silu_all, f * rows, rows, 1)
    partial = dot(silu_own, modulation_weight[0])
    bias_row = lax.dynamic_update_slice_in_dim(
        jnp.zeros((1, 6 * width), f32),
        modulation_bias.astype(f32),
        f * modulation_bias.shape[1],
        1,
    )
    modulation = small_reduce(partial + bias_row, "fsdp")
    shift_attn, scale_attn, gate_attn, shift_mlp, scale_mlp, gate_mlp = [
        modulation[:, at * width : (at + 1) * width] for at in range(6)
    ]

    norm_attn, inv_attn = layer_norm(hidden)
    low_attn = (norm_attn * (1.0 + scale_attn) + shift_attn).astype(bf16)
    low_attn, forward_own = tie(low_attn, forward_own)
    input_attn = seq_gather(low_attn)
    forward_full = lax.all_gather(forward_own, "fsdp", axis=1, tiled=True)
    fc1_full, fc2_full = forward_full[0], forward_full[1]
    d_result = upstream * gate_mlp
    low_result, packed_weight = tie(d_result.astype(bf16), qkv_full)
    d_result_low = seq_gather(low_result)

    query_bias = lax.dynamic_slice_in_dim(qkv_offset[:, :width], s * group, group, 1)
    value_bias = lax.dynamic_slice_in_dim(qkv_offset[:, width:], s * group, group, 1)
    zeros = jnp.zeros((1, group), f32)
    offsets = jnp.concatenate(
        [query_bias, zeros, value_bias, zeros[:, : padded - 3 * group]], axis=1
    )
    packed = (dot(input_attn, packed_weight) + offsets).astype(bf16)
    length = packed.shape[0]
    heads = packed[:, : 3 * group].reshape(length, 3, local_heads, head_width)
    queries, key_rows, value_rows = heads[:, 0], heads[:, 1], heads[:, 2]
    scores = (
        jnp.einsum("qhd,khd->hqk", queries, key_rows, preferred_element_type=f32) * score_scale
    )
    row_peak = jnp.max(scores, axis=-1, keepdims=True)
    log_total = jnp.log(jnp.sum(jnp.exp(scores - row_peak), axis=-1, keepdims=True)) + row_peak
    probabilities = jnp.exp(scores - log_total)
    prob_low = probabilities.astype(bf16)
    attended = jnp.einsum("hqk,khd->qhd", prob_low, value_rows, preferred_element_type=f32).astype(
        bf16
    )
    attended_flat = attended.reshape(length, group)
    branch_part = dot(attended_flat, proj_full)
    branch = seq_reduce(branch_part) + proj_offset
    middle = hidden + gate_attn * branch

    norm_mlp, inv_mlp = layer_norm(middle)
    low_mlp = (norm_mlp * (1.0 + scale_mlp) + shift_mlp).astype(bf16)
    low_mlp, d_result_low = tie(low_mlp, d_result_low)
    input_mlp = seq_gather(low_mlp)
    fc1_offset_own = lax.dynamic_index_in_dim(
        fc1_offset.reshape(fsdp, seq, quarter), s, 1, keepdims=False
    ).reshape(1, units)
    before = dot(input_mlp, fc1_full) + fc1_offset_own
    activated, pullback = jax.vjp(gelu_tanh, before)
    act_low = activated.astype(bf16)
    d_before = pullback(dot_back(d_result_low, fc2_full))[0]
    d_before_low = d_before.astype(bf16)
    fc2_near = reduce_near(dot_rows(act_low, d_result_low))
    d_input_part = dot_back(d_before_low, fc1_full)
    fc1_near = reduce_near(dot_rows(input_mlp, d_before_low))
    d_input_part, act_late = tie(d_input_part, act_low)
    d_input_mlp = seq_reduce(d_input_part)
    result = seq_reduce(dot(act_late, fc2_full)) + fc2_offset
    output = middle + gate_mlp * result
    d_gate_mlp = jnp.sum(upstream * result, axis=0, keepdims=True)
    fc2_bias_part = jnp.sum(d_result, axis=0, keepdims=True)
    fc1_bias_part = jnp.sum(d_before, axis=0, keepdims=True)
    d_scale_mlp = jnp.sum(d_input_mlp * norm_mlp, axis=0, keepdims=True)
    d_shift_mlp = jnp.sum(d_input_mlp, axis=0, keepdims=True)
    d_middle = upstream + norm_back(d_input_mlp * (1.0 + scale_mlp), norm_mlp, inv_mlp)

    d_branch = d_middle * gate_attn
    d_gate_attn = jnp.sum(d_middle * branch, axis=0, keepdims=True)
    proj_bias_part = jnp.sum(d_branch, axis=0, keepdims=True)
    low_branch = d_branch.astype(bf16)
    d_branch_low = seq_gather(low_branch)
    fc2_grad = reduce_far(*fc2_near)
    proj_grad = split_columns(dot_rows(attended_flat, d_branch_low).astype(bf16), s, seq)
    proj_grad, d_branch_low = tie(proj_grad, d_branch_low)
    proj_grad = seq_exchange([proj_grad[k] for k in range(seq)])
    d_attended = dot_back(d_branch_low, proj_full).astype(bf16).reshape(attended.shape)
    d_probs = jnp.einsum("qhd,khd->hqk", d_attended, value_rows, preferred_element_type=f32)
    delta = jnp.sum(d_attended.astype(f32) * attended.astype(f32), axis=-1).T
    d_scores = (probabilities * (d_probs - delta[..., None]) * score_scale).astype(bf16)
    d_queries = jnp.einsum("hqk,khd->qhd", d_scores, key_rows, preferred_element_type=f32)
    d_keys = jnp.einsum("hqk,qhd->khd", d_scores, queries, preferred_element_type=f32)
    d_values = jnp.einsum("hqk,qhd->khd", prob_low, d_attended, preferred_element_type=f32)
    d_packed = jnp.concatenate(
        [grad.astype(bf16).reshape(length, group) for grad in (d_queries, d_keys, d_values)]
        + [jnp.zeros((length, padded - 3 * group), bf16)],
        axis=1,
    )
    d_input_part = dot_back(d_packed, qkv_full)
    d_input_attn = seq_reduce(d_input_part)
    fc1_grad = reduce_far(*fc1_near)
    qkv_grad = dot_rows(input_attn, d_packed).astype(bf16)
    qkv_near = reduce_near(qkv_grad)
    proj_near = reduce_near(join_rows(proj_grad, s, bf16))
    qkv_sum = jnp.sum(d_packed.astype(f32), axis=0, keepdims=True)
    d_scale_attn = jnp.sum(d_input_attn * norm_attn, axis=0, keepdims=True)
    d_shift_attn = jnp.sum(d_input_attn, axis=0, keepdims=True)
    latents_grad = d_middle + norm_back(d_input_attn * (1.0 + scale_attn), norm_attn, inv_attn)

    sums = seq_sum(
        jnp.concatenate(
            [
                d_shift_attn,
                d_scale_attn,
                d_gate_attn,
                d_shift_mlp,
                d_scale_mlp,
                d_gate_mlp,
                proj_bias_part,
                fc2_bias_part,
            ],
            axis=1,
        )
    )
    own_columns = jnp.concatenate(
        [qkv_sum[:, :group], qkv_sum[:, 2 * group : 3 * group], fc1_bias_part], axis=1
    )
    columns = small_gather(own_columns, "seq")
    query_sum = columns[:, :group].reshape(1, -1)
    value_sum = columns[:, group : 2 * group].reshape(1, -1)
    fc1_sum = jnp.moveaxis(columns[:, 2 * group :].reshape(seq, fsdp, quarter), 0, 1).reshape(1, -1)
    every = small_gather(
        jnp.concatenate([sums, query_sum, value_sum, fc1_sum], axis=1), "fsdp"
    )
    every, *qkv_near = tie(every, *qkv_near)
    d_modulation = every[:, : 6 * width]
    weight_grad = lax.dot_general(
        silu_own.astype(f32),
        d_modulation,
        (((0,), (0,)), ((), ())),
        precision=lax.Precision.HIGHEST,
    )
    totals = jnp.sum(every, axis=0, keepdims=True)

    def own_part(start, count):
        part = count // fsdp
        return lax.dynamic_slice_in_dim(totals[:, start : start + count], f * part, part, 1)

    modulation_bias_grad = own_part(0, 6 * width)
    proj_bias_grad = own_part(6 * width, width)
    fc2_bias_grad = own_part(7 * width, width)
    qkv_bias_grad = own_part(8 * width, 2 * width)
    fc1_bias_grad = own_part(10 * width, fc1_offset.shape[1])

    cond_rows = lax.dot_general(
        d_modulation,
        modulation_weight[0].astype(f32),
        (((1,), (1,)), ((), ())),
        precision=lax.Precision.HIGHEST,
    )
    cond_all = small_gather(cond_rows.reshape(1, -1), "fsdp").reshape(fsdp, fsdp, rows)
    cond_sum = lax.dynamic_index_in_dim(cond_all, f, 1, keepdims=False).reshape(1, width)
    conditioning_grad = jax.vjp(jax.nn.silu, conditioning)[1](cond_sum)[0]

    fc2_out = join_rows(seq_blocks(fc2_grad.astype(bf16)), s, f32)
    fc1_out = join_columns(seq_blocks(fc1_grad.astype(bf16)), s, fsdp, quarter, f32)
    proj_grad = reduce_far(*proj_near)
    qkv_grad = reduce_far(*qkv_near)
    proj_out = join_columns(seq_blocks(proj_grad.astype(bf16)), s, 1, group, f32)
    qkv_out = join_columns(seq_blocks(qkv_grad.astype(bf16)), s, 3, group, f32)
    return (
        output[None],
        latents_grad[None],
        conditioning_grad,
        weight_grad[None],
        modulation_bias_grad,
        qkv_out[None],
        qkv_bias_grad,
        proj_out[None],
        proj_bias_grad,
        fc1_out[None],
        fc1_bias_grad,
        fc2_out[None],
        fc2_bias_grad,
    )


def solution(mesh):
    tokens = P("fsdp", "seq", None)
    matrix = P(None, "fsdp", None)
    vector = P(None, "fsdp")
    cond = P("fsdp", None)
    weights = (matrix, vector) * 5

    return jax.shard_map(
        shards,
        mesh=mesh,
        in_specs=(tokens, cond) + weights + (tokens,),
        out_specs=(tokens, tokens, cond) + weights,
        check_vma=False,
    )
```

```python
import jax
import jax.numpy as jnp
from jax import lax
from jax.experimental import pallas as pl
from jax.experimental.pallas import tpu as pltpu
from jax.sharding import PartitionSpec as P


HEADS = 16
NORM_EPS = 1e-06


def layer_norm(hidden):
    center = hidden - jnp.mean(hidden, axis=-1, keepdims=True)
    inverse = lax.rsqrt(jnp.mean(center * center, axis=-1, keepdims=True) + NORM_EPS)
    return (center * inverse, inverse)


def norm_back(upstream, normed, inverse):
    return inverse * (
        upstream
        - jnp.mean(upstream, axis=-1, keepdims=True)
        - normed * jnp.mean(upstream * normed, axis=-1, keepdims=True)
    )


def gelu_tanh(before):
    return jax.nn.gelu(before, approximate=True)


def dot(left, right):
    return jnp.dot(left, right, preferred_element_type=jnp.float32)


def dot_back(left, weight):
    return lax.dot_general(
        left, weight, (((left.ndim - 1,), (1,)), ((), ())), preferred_element_type=jnp.float32
    )


def dot_rows(left, right):
    return lax.dot_general(left, right, (((0,), (0,)), ((), ())), preferred_element_type=jnp.float32)


def swap(value, axis, mask):
    pairs = [(i, i ^ mask) for i in range(lax.axis_size(axis))]
    return lax.ppermute(value, axis, pairs)


def bits_of(size):
    bits = []
    step = 1
    while step < size:
        bits.append(step)
        step *= 2
    return bits


def seq_gather(value):
    return jnp.concatenate(seq_blocks(value), axis=0)


def seq_blocks(value):
    blocks = {0: value}
    for mask in reversed(bits_of(lax.axis_size("seq"))):
        for tag in list(blocks):
            blocks[tag ^ mask] = swap(blocks[tag], "seq", mask)
    return [blocks[tag] for tag in range(len(blocks))]


def seq_exchange(blocks):
    count = len(blocks)
    blocks = list(blocks)
    for mask in bits_of(count):
        kept = [tag for tag in range(count) if not tag & mask]
        received = swap(jnp.stack([blocks[tag | mask] for tag in kept]), "seq", mask)
        moved = {tag | mask: received[at] for at, tag in enumerate(kept)}
        blocks = [moved.get(tag, blocks[tag]) for tag in range(count)]
    return blocks


def seq_reduce(partial):
    size = lax.axis_size("seq")
    rows = partial.shape[0] // size
    for mask in bits_of(size):
        count = partial.shape[0] // rows
        blocks = partial.reshape((count // 2, 2) + (rows,) + partial.shape[1:])
        kept, sent = blocks[:, 0], blocks[:, 1]
        received = swap(sent.astype(jnp.bfloat16), "seq", mask)
        partial = (kept + received.astype(jnp.float32)).reshape((-1,) + partial.shape[1:])
    return partial


def tie(*values):
    return lax.optimization_barrier(values)


def fsdp_gather(block):
    own = lax.axis_index("fsdp")
    count = lax.axis_size("fsdp") // 2
    stack = jnp.zeros((count,) + block.shape, block.dtype)
    for k in range(count):
        part = swap(block, "fsdp", 2 * k) if k else block
        stack = lax.dynamic_update_slice_in_dim(stack, part[None], (own // 2) ^ k, 0)
    other = swap(stack, "fsdp", 1)
    upper = own % 2 == 1
    first = jnp.where(upper, other, stack)
    second = jnp.where(upper, stack, other)
    return jnp.stack([first, second], axis=1).reshape((-1,) + block.shape[1:])


def reduce_near(partial):
    size = lax.axis_size("fsdp")
    near = lax.axis_index("fsdp") % 2
    rows = partial.shape[0] // size
    blocks = partial.astype(jnp.bfloat16).reshape((size // 2, 2, rows) + partial.shape[1:])
    kept = lax.dynamic_index_in_dim(blocks, near, 1, keepdims=False)
    sent = lax.dynamic_index_in_dim(blocks, 1 - near, 1, keepdims=False)
    return (kept, swap(sent, "fsdp", 1))


def reduce_far(kept, received):
    far = lax.axis_index("fsdp") // 2
    pair = kept.astype(jnp.float32) + received.astype(jnp.float32)
    total = lax.dynamic_index_in_dim(pair, far, 0, keepdims=False)
    low = pair.astype(jnp.bfloat16)
    received = []
    for k in range(1, pair.shape[0]):
        piece = lax.dynamic_index_in_dim(low, far ^ k, 0, keepdims=False)
        received.append(swap(piece, "fsdp", 2 * k))
    for part in received:
        total = total + part.astype(jnp.float32)
    return total.astype(jnp.bfloat16)


def lanes(columns):
    return -(-columns // 128) * 128


def in_vmem(count):
    return [pl.BlockSpec(memory_space=pltpu.VMEM) for _ in range(count)]


def own_columns_of(whole, part, groups, parts):
    span = whole.shape[1] // (groups * parts)
    starts = [(group * parts + part) * span for group in range(groups)]
    return [whole[:, start : start + span] for start in starts]


def take_attention(qkv, proj, index, parts):
    rows = qkv.shape[0]
    used = qkv.shape[1] // parts

    def kernel(at_ref, qkv_ref, proj_ref, target, proj_target):
        for part in range(parts):

            @pl.when(at_ref[0] == part)
            def _():
                pieces = own_columns_of(qkv_ref[...], part, 3, parts)
                pieces.append(jnp.zeros((rows, lanes(used) - used), qkv.dtype))
                target[...] = jnp.concatenate(pieces, axis=1)
                proj_target[...] = own_columns_of(proj_ref[...], part, 1, parts)[0]

    return pl.pallas_call(
        kernel,
        out_shape=[
            jax.ShapeDtypeStruct((rows, lanes(used)), qkv.dtype),
            jax.ShapeDtypeStruct((rows, proj.shape[1] // parts), proj.dtype),
        ],
        in_specs=[pl.BlockSpec(memory_space=pltpu.SMEM)] + in_vmem(2),
        out_specs=in_vmem(2),
    )(index.reshape(1), qkv, proj)


def take_feed_forward(fc1, fc2, index, groups, parts):
    rows, width = fc1.shape[0], fc2.shape[1]
    quarter = fc2.shape[0] // parts

    def kernel(at_ref, fc1_ref, fc2_ref, target):
        for part in range(parts):

            @pl.when(at_ref[0] == part)
            def _():
                pieces = own_columns_of(fc1_ref[...], part, groups, parts)
                target[0] = jnp.concatenate(pieces, axis=1)
                target[1] = fc2_ref[part * quarter : (part + 1) * quarter]

    return pl.pallas_call(
        kernel,
        out_shape=jax.ShapeDtypeStruct((2, rows, width), fc1.dtype),
        in_specs=[pl.BlockSpec(memory_space=pltpu.SMEM)] + in_vmem(2),
        out_specs=in_vmem(1)[0],
    )(index.reshape(1), fc1, fc2)


def pick(refs, index, dtype):
    value = refs[0][...]
    for at in range(1, len(refs)):
        value = jnp.where(index == at, refs[at][...], value)
    return value.astype(dtype)


def split_columns(whole, index, parts):
    rows, columns = whole.shape
    span = columns // parts

    def kernel(at_ref, source, target):
        for own in range(parts):

            @pl.when(at_ref[0] == own)
            def _():
                values = source[...]
                for part in range(parts):
                    start = (own ^ part) * span
                    target[part] = values[:, start : start + span]

    return pl.pallas_call(
        kernel,
        out_shape=jax.ShapeDtypeStruct((parts, rows, span), whole.dtype),
        in_specs=[pl.BlockSpec(memory_space=pltpu.SMEM)] + in_vmem(1),
        out_specs=in_vmem(1)[0],
    )(index.reshape(1), whole)


def join_columns(blocks, index, groups, span, dtype):
    parts, rows = len(blocks), blocks[0].shape[0]

    def kernel(at_ref, *refs):
        target = refs[-1]
        wholes = [pick(refs[:-1], at_ref[0] ^ part, dtype) for part in range(parts)]
        pieces = []
        for group in range(groups):
            for part in range(parts):
                pieces.append(wholes[part][:, group * span : (group + 1) * span])
        target[...] = jnp.concatenate(pieces, axis=1)

    return pl.pallas_call(
        kernel,
        out_shape=jax.ShapeDtypeStruct((rows, parts * groups * span), dtype),
        in_specs=[pl.BlockSpec(memory_space=pltpu.SMEM)] + in_vmem(parts),
        out_specs=in_vmem(1)[0],
    )(index.reshape(1), *blocks)


def join_rows(blocks, index, dtype):
    parts = len(blocks)
    rows, columns = blocks[0].shape

    def kernel(at_ref, *refs):
        target = refs[-1]
        for part in range(parts):
            value = pick(refs[:-1], at_ref[0] ^ part, dtype)
            target[part * rows : (part + 1) * rows] = value

    return pl.pallas_call(
        kernel,
        out_shape=jax.ShapeDtypeStruct((parts * rows, columns), dtype),
        in_specs=[pl.BlockSpec(memory_space=pltpu.SMEM)] + in_vmem(parts),
        out_specs=in_vmem(1)[0],
    )(index.reshape(1), *blocks)


def small_gather(row, axis):
    own = lax.axis_index(axis)
    rows = row
    for mask in bits_of(lax.axis_size(axis)):
        other = swap(rows, axis, mask)
        upper = (own & mask) != 0
        rows = jnp.concatenate(
            [jnp.where(upper, other, rows), jnp.where(upper, rows, other)], axis=0
        )
    return rows


def small_reduce(rows, axis):
    own = lax.axis_index(axis)
    for mask in bits_of(lax.axis_size(axis)):
        pairs = rows.reshape(rows.shape[0] // 2, 2, rows.shape[1])
        upper = (own & mask) != 0
        kept = jnp.where(upper, pairs[:, 1], pairs[:, 0])
        sent = jnp.where(upper, pairs[:, 0], pairs[:, 1])
        rows = kept + swap(sent, axis, mask)
    return rows


def seq_sum(value):
    for mask in bits_of(lax.axis_size("seq")):
        value = value + swap(value, "seq", mask)
    return value


def shards(
    latents,
    conditioning,
    modulation_weight,
    modulation_bias,
    qkv_weight,
    qkv_bias,
    proj_weight,
    proj_bias,
    fc1_weight,
    fc1_bias,
    fc2_weight,
    fc2_bias,
    cotangent,
):
    f32, bf16 = jnp.float32, jnp.bfloat16
    seq, fsdp = lax.axis_size("seq"), lax.axis_size("fsdp")
    s, f = lax.axis_index("seq"), lax.axis_index("fsdp")
    hidden = latents[0].astype(f32)
    upstream = cotangent[0]
    width = hidden.shape[1]
    group = width // seq
    head_width = width // HEADS
    local_heads = HEADS // seq
    rows = qkv_weight.shape[1]
    unit_rows = fc2_weight.shape[1]
    quarter = unit_rows // seq
    units = quarter * fsdp
    score_scale = head_width ** (-0.5)

    attention_own, proj_own = take_attention(qkv_weight[0], proj_weight[0], s, seq)
    attention_own, vector = tie(attention_own, conditioning)
    silu_cond = jax.nn.silu(vector).astype(bf16)
    shorts = [silu_cond, qkv_bias, proj_bias, fc1_bias, fc2_bias]
    gathered = small_gather(jnp.concatenate(shorts, axis=1), "fsdp")
    split = []
    at = 0
    for short in shorts:
        split.append(gathered[:, at : at + short.shape[1]])
        at += short.shape[1]
    silu_all = split[0]
    qkv_offset, proj_offset, fc1_offset, fc2_offset = [
        part.astype(f32).reshape(1, -1) for part in split[1:]
    ]

    qkv_full = lax.all_gather(attention_own, "fsdp", axis=0, tiled=True)
    padded = lanes(3 * group)
    forward_own = take_feed_forward(fc1_weight[0], fc2_weight[0], s, fsdp, seq)

    silu_own = lax.dynamic_slice_in_dim(silu_all, f * rows, rows, 1)
    partial = dot(silu_own, modulation_weight[0])
    bias_row = lax.dynamic_update_slice_in_dim(
        jnp.zeros((1, 6 * width), f32),
        modulation_bias.astype(f32),
        f * modulation_bias.shape[1],
        1,
    )
    modulation = small_reduce(partial + bias_row, "fsdp")
    shift_attn, scale_attn, gate_attn, shift_mlp, scale_mlp, gate_mlp = [
        modulation[:, at * width : (at + 1) * width] for at in range(6)
    ]

    norm_attn, inv_attn = layer_norm(hidden)
    low_attn = (norm_attn * (1.0 + scale_attn) + shift_attn).astype(bf16)
    low_attn, forward_own, proj_own = tie(low_attn, forward_own, proj_own)
    input_attn = seq_gather(low_attn)
    proj_blocks = fsdp_gather(proj_own).reshape(seq, group, group)
    proj_blocks = [
        lax.dynamic_index_in_dim(proj_blocks, s ^ k, 0, keepdims=False) for k in range(seq)
    ]
    proj_full = join_columns(seq_exchange(proj_blocks), s, 1, group, bf16)
    forward_full = lax.all_gather(forward_own, "fsdp", axis=1, tiled=True)
    fc1_full, fc2_full = forward_full[0], forward_full[1]
    d_result = upstream * gate_mlp
    low_result, packed_weight = tie(d_result.astype(bf16), qkv_full)
    d_result_low = seq_gather(low_result)

    query_bias = lax.dynamic_slice_in_dim(qkv_offset[:, :width], s * group, group, 1)
    value_bias = lax.dynamic_slice_in_dim(qkv_offset[:, width:], s * group, group, 1)
    zeros = jnp.zeros((1, group), f32)
    offsets = jnp.concatenate(
        [query_bias, zeros, value_bias, zeros[:, : padded - 3 * group]], axis=1
    )
    packed = (dot(input_attn, packed_weight) + offsets).astype(bf16)
    length = packed.shape[0]
    heads = packed[:, : 3 * group].reshape(length, 3, local_heads, head_width)
    queries, key_rows, value_rows = heads[:, 0], heads[:, 1], heads[:, 2]
    scores = (
        jnp.einsum("qhd,khd->hqk", queries, key_rows, preferred_element_type=f32) * score_scale
    )
    row_peak = jnp.max(scores, axis=-1, keepdims=True)
    log_total = jnp.log(jnp.sum(jnp.exp(scores - row_peak), axis=-1, keepdims=True)) + row_peak
    probabilities = jnp.exp(scores - log_total)
    prob_low = probabilities.astype(bf16)
    attended = jnp.einsum("hqk,khd->qhd", prob_low, value_rows, preferred_element_type=f32).astype(
        bf16
    )
    attended_flat = attended.reshape(length, group)
    branch_part = dot(attended_flat, proj_full)
    branch = seq_reduce(branch_part) + proj_offset
    middle = hidden + gate_attn * branch

    norm_mlp, inv_mlp = layer_norm(middle)
    low_mlp = (norm_mlp * (1.0 + scale_mlp) + shift_mlp).astype(bf16)
    low_mlp, d_result_low = tie(low_mlp, d_result_low)
    input_mlp = seq_gather(low_mlp)
    fc1_offset_own = lax.dynamic_index_in_dim(
        fc1_offset.reshape(fsdp, seq, quarter), s, 1, keepdims=False
    ).reshape(1, units)
    before = dot(input_mlp, fc1_full) + fc1_offset_own
    activated, pullback = jax.vjp(gelu_tanh, before)
    act_low = activated.astype(bf16)
    d_activated = dot_back(d_result_low, fc2_full)
    d_before = pullback(d_activated)[0]
    d_before_low = d_before.astype(bf16)
    fc2_near = reduce_near(dot_rows(act_low, d_result_low))
    d_input_part = dot_back(d_before_low, fc1_full)
    fc1_near = reduce_near(dot_rows(input_mlp, d_before_low))
    d_input_part, act_late = tie(d_input_part, act_low)
    d_input_mlp = seq_reduce(d_input_part)
    result = seq_reduce(dot(act_late, fc2_full)) + fc2_offset
    fc2_bias_part = jnp.sum(d_result, axis=0, keepdims=True)
    fc1_bias_part = jnp.sum(d_before, axis=0, keepdims=True)
    d_scale_mlp = jnp.sum(d_input_mlp * norm_mlp, axis=0, keepdims=True)
    d_shift_mlp = jnp.sum(d_input_mlp, axis=0, keepdims=True)
    d_middle = upstream + norm_back(d_input_mlp * (1.0 + scale_mlp), norm_mlp, inv_mlp)

    d_branch = d_middle * gate_attn
    d_gate_attn = jnp.sum(d_middle * branch, axis=0, keepdims=True)
    proj_bias_part = jnp.sum(d_branch, axis=0, keepdims=True)
    low_branch = d_branch.astype(bf16)
    low_branch, late_upstream, late_middle = tie(low_branch, upstream, middle)
    output = late_middle + gate_mlp * result
    d_gate_mlp = jnp.sum(late_upstream * result, axis=0, keepdims=True)
    d_branch_low = seq_gather(low_branch)
    fc2_grad = reduce_far(*fc2_near)
    proj_grad = split_columns(dot_rows(attended_flat, d_branch_low).astype(bf16), s, seq)
    proj_grad, d_branch_low = tie(proj_grad, d_branch_low)
    proj_grad = seq_exchange([proj_grad[k] for k in range(seq)])
    d_attended = dot_back(d_branch_low, proj_full).astype(bf16).reshape(attended.shape)
    d_probs = jnp.einsum("qhd,khd->hqk", d_attended, value_rows, preferred_element_type=f32)
    delta = jnp.sum(d_attended.astype(f32) * attended.astype(f32), axis=-1).T
    d_scores = (probabilities * (d_probs - delta[..., None]) * score_scale).astype(bf16)
    d_queries = jnp.einsum("hqk,khd->qhd", d_scores, key_rows, preferred_element_type=f32)
    d_keys = jnp.einsum("hqk,qhd->khd", d_scores, queries, preferred_element_type=f32)
    d_values = jnp.einsum("hqk,qhd->khd", prob_low, d_attended, preferred_element_type=f32)
    d_packed = jnp.concatenate(
        [grad.astype(bf16).reshape(length, group) for grad in (d_queries, d_keys, d_values)]
        + [jnp.zeros((length, padded - 3 * group), bf16)],
        axis=1,
    )
    d_input_part = dot_back(d_packed, qkv_full)
    d_input_attn = seq_reduce(d_input_part)
    fc1_grad = reduce_far(*fc1_near)
    qkv_grad = dot_rows(input_attn, d_packed).astype(bf16)
    qkv_near = reduce_near(qkv_grad)
    proj_near = reduce_near(join_rows(proj_grad, s, bf16))
    qkv_sum = jnp.sum(d_packed.astype(f32), axis=0, keepdims=True)
    d_scale_attn = jnp.sum(d_input_attn * norm_attn, axis=0, keepdims=True)
    d_shift_attn = jnp.sum(d_input_attn, axis=0, keepdims=True)
    latents_grad = d_middle + norm_back(d_input_attn * (1.0 + scale_attn), norm_attn, inv_attn)

    parts = [
        d_shift_attn,
        d_scale_attn,
        d_gate_attn,
        d_shift_mlp,
        d_scale_mlp,
        d_gate_mlp,
        proj_bias_part,
        fc2_bias_part,
    ]
    sums = seq_sum(jnp.concatenate(parts, axis=1))
    own_columns = jnp.concatenate(
        [qkv_sum[:, :group], qkv_sum[:, 2 * group : 3 * group], fc1_bias_part], axis=1
    )
    columns = small_gather(own_columns, "seq")
    query_sum = columns[:, :group].reshape(1, -1)
    value_sum = columns[:, group : 2 * group].reshape(1, -1)
    fc1_sum = jnp.moveaxis(columns[:, 2 * group :].reshape(seq, fsdp, quarter), 0, 1).reshape(1, -1)
    row = jnp.concatenate([sums, query_sum, value_sum, fc1_sum], axis=1)
    every = small_gather(row.astype(bf16), "fsdp")
    every, *qkv_near = tie(every, *qkv_near)
    every = every.astype(f32)
    d_modulation = every[:, : 6 * width]
    weight_grad = lax.dot_general(
        silu_own.astype(f32),
        d_modulation,
        (((0,), (0,)), ((), ())),
        precision=lax.Precision.HIGHEST,
    )
    totals = jnp.sum(every, axis=0, keepdims=True)

    def own_part(start, count):
        part = count // fsdp
        return lax.dynamic_slice_in_dim(totals[:, start : start + count], f * part, part, 1)

    modulation_bias_grad = own_part(0, 6 * width)
    proj_bias_grad = own_part(6 * width, width)
    fc2_bias_grad = own_part(7 * width, width)
    qkv_bias_grad = own_part(8 * width, 2 * width)
    fc1_bias_grad = own_part(10 * width, fc1_offset.shape[1])

    cond_rows = lax.dot_general(
        d_modulation,
        modulation_weight[0].astype(f32),
        (((1,), (1,)), ((), ())),
        precision=lax.Precision.HIGHEST,
    )
    cond_all = small_gather(cond_rows.reshape(1, -1), "fsdp").reshape(fsdp, fsdp, rows)
    cond_sum = lax.dynamic_index_in_dim(cond_all, f, 1, keepdims=False).reshape(1, width)
    conditioning_grad = jax.vjp(jax.nn.silu, conditioning)[1](cond_sum)[0]

    fc2_out = join_rows(seq_blocks(fc2_grad), s, f32)
    fc1_out = join_columns(seq_blocks(fc1_grad), s, fsdp, quarter, f32)
    proj_grad = reduce_far(*proj_near)
    qkv_grad = reduce_far(*qkv_near)
    proj_out = join_columns(seq_blocks(proj_grad), s, 1, group, f32)
    qkv_out = join_columns(seq_blocks(qkv_grad), s, 3, group, f32)
    return (
        output[None],
        latents_grad[None],
        conditioning_grad,
        weight_grad[None],
        modulation_bias_grad,
        qkv_out[None],
        qkv_bias_grad,
        proj_out[None],
        proj_bias_grad,
        fc1_out[None],
        fc1_bias_grad,
        fc2_out[None],
        fc2_bias_grad,
    )


def solution(mesh):
    tokens = P("fsdp", "seq", None)
    matrix = P(None, "fsdp", None)
    vector = P(None, "fsdp")
    cond = P("fsdp", None)
    weights = (matrix, vector) * 5

    return jax.shard_map(
        shards,
        mesh=mesh,
        in_specs=(tokens, cond) + weights + (tokens,),
        out_specs=(tokens, tokens, cond) + weights,
        check_vma=False,
    )
```
